32 devices in a mesh: sec: 2 (over core), row: 4 (over y, x), col: 4 (over z).
Axes of the slice: x: 2, y: 2, z: 4, core: 2. Of those that a mesh axis runs over, the one named last changes fastest.
Arguments:
- anc_inverse: float32 [2048, 2048], P('row', ('sec', 'col')), as said below
- panel: float32 [8192, 2048], P(('sec', 'col'), 'row'), may hold values from -0.5 to 0.5
- diag_inverse: float32 [8192, 512], P(('sec', 'col')), may hold values from -6 to 6
- widths: int32 [16], replicated, may hold values from 1 to 4, as said below
- pattern: int32 [16, 16], replicated, may hold values 0 or 1
Outputs:
- off_inverse: float32 [8192, 2048], P(('sec', 'col'), 'row')
- child_inverse: float32 [8192, 512], P(('sec', 'col'))
The draws below stay inside these ranges and needn't reach their ends.
Inputs may be any that keep to these rules, and one draw needn't show every extreme that they name: `anc_inverse`: exactly symmetric. `widths`: both 1 and 4 occur in every draw.
All inputs are finite; a program needn't handle non-finite values.
Results may differ from the reference program's by a relative error of at most 0.0003.
Values sent between devices are 32-bit elements; how exact they have to be, the bound alone decides.
A program may use at most 128 MiB of HBM per device.

```python
import math
import jax
import jax.numpy as jnp
from jax import lax

B = 128
WMAX = 4
SW = 512
NA = 2048
NAB = 16
SLOTS = 16
CHILD_COLS = 8192


def draw_anc_inverse(key, part):
    first_key, second_key = jax.random.split(jax.random.fold_in(key, 11), 2)
    rough = jax.random.normal(first_key, (NA, NA), jnp.float32)
    symmetric = (rough + rough.T) * (0.5 ** 0.5 / math.sqrt(NA))
    diagonal = jnp.exp(jax.random.uniform(second_key, (NA,), jnp.float32, 0.0, math.log(4.0)))
    return symmetric + jnp.diag(diagonal)


def draw_widths(key, part):
    first_key, second_key = jax.random.split(jax.random.fold_in(key, 23))
    drawn = jax.random.randint(first_key, (SLOTS,), 1, WMAX + 1)
    spots = jax.random.permutation(second_key, SLOTS)
    drawn = drawn.at[spots[0]].set(WMAX).at[spots[1]].set(1)
    return drawn.astype(jnp.int32)


def touch_ends(entries, own_key, smallest, largest):
    place = [jax.random.randint(jax.random.fold_in(own_key, axis), (), 0, length) for axis, length in enumerate(entries.shape)]
    longest = entries.shape.index(max(entries.shape))
    neighbour = place[:longest] + [(place[longest] + 1) % entries.shape[longest]] + place[longest + 1:]
    return entries.at[tuple(place)].set(smallest).at[tuple(neighbour)].set(largest)


def levels(key, extent, cuts, low, largest):
    level = 1.0
    for axis_at, blocks in cuts:
        draws = jax.random.uniform(jax.random.fold_in(jax.random.fold_in(key, 6), axis_at), (blocks,), jnp.float32, low / len(cuts), largest / len(cuts))
        level = level * jnp.repeat(jnp.exp(draws), extent[axis_at] // blocks).reshape((-1,) + (1,) * (len(extent) - 1 - axis_at))
    return level


def gaussian(rng, shape, deviation, most, shards=(), kind=jnp.bfloat16):
    result = jax.random.normal(rng, shape, jnp.float32) * deviation
    if len(shards) > 0:
        result = levels(rng, shape, shards, -0.22, 0.18) * result
    return jnp.clip(result, min=-most, max=most).astype(kind)


def setup_inputs(seed: int = 0) -> dict:
    key_list = jax.random.split(jax.random.key(seed), 6)
    return {
        "anc_inverse": draw_anc_inverse(jax.random.fold_in(key_list[5], 71), 0),
        "panel": gaussian(key_list[1], (CHILD_COLS, NA), (NA // 16) ** -0.5, 0.5, ((0, 8), (1, 4)), jnp.float32),
        "diag_inverse": gaussian(key_list[2], (CHILD_COLS, SW), 1.0, 6.0, ((0, 8),), jnp.float32),
        "widths": draw_widths(jax.random.fold_in(key_list[5], 71), 0),
        "pattern": touch_ends((jax.random.randint(key_list[4], (SLOTS, NAB), 0, 2) < 1).astype(jnp.int32), jax.random.fold_in(key_list[4], 1), 0, 1),
    }


def reference(anc_inverse, panel, diag_inverse, widths, pattern):
    highest = lax.Precision.HIGHEST
    position = jnp.arange(SW, dtype=jnp.int32)

    def solve_slot(inputs):
        slot_panel, slot_diag, slot_blocks, slot_pattern = inputs
        column_mask = (position < slot_blocks * B).astype(jnp.float32)
        row_mask = jnp.repeat(slot_pattern.astype(jnp.float32), B)
        masked = slot_panel * column_mask[:, None] * row_mask[None, :]
        product = jnp.dot(masked, anc_inverse, precision=highest, preferred_element_type=jnp.float32)
        product = product * column_mask[:, None] * row_mask[None, :]
        update = jnp.dot(product, masked.T, precision=highest, preferred_element_type=jnp.float32)
        diag_block = (slot_diag + update) * column_mask[:, None] * column_mask[None, :]
        return -product, diag_block

    off_blocks, diag_blocks = lax.map(
        solve_slot,
        (panel.reshape(SLOTS, SW, NA), diag_inverse.reshape(SLOTS, SW, SW), widths, pattern),
    )
    return off_blocks.reshape(SLOTS * SW, NA), diag_blocks.reshape(SLOTS * SW, SW)
```

```python
import functools
import jax
import jax.numpy as jnp
from jax import lax
from jax.experimental import pallas as pl
from jax.experimental.pallas import tpu as pltpu
from jax.sharding import PartitionSpec as P

B = 128
SW = 512
F32 = jnp.float32
BF = jnp.bfloat16
MESH = pl.DeviceIdType.MESH
NN = (((1,), (0,)), ((), ()))
NT = (((1,), (1,)), ((), ()))


def split(value):
    high = value.astype(BF)
    return high, (value - high.astype(F32)).astype(BF)


def dot3(ah, al, bh, bl, dims):
    dot = functools.partial(lax.dot_general, dimension_numbers=dims, preferred_element_type=F32)
    return dot(ah, bh) + (dot(ah, bl) + dot(al, bh))


def factor(count):
    low = 1
    for value in range(1, count + 1):
        if count % value == 0 and value * value <= count:
            low = value
    return count // low, low


def kernel(
    sizes,
    anc_ref, panel_ref, prod_ref, upd_ref,
    anc, ah, al, ph, plo, pin, opp, oh, ol, qsend, qrecv, upack, urecv, usum, ugat,
    zs, zr, ps, pr, os_, or_, qs, qr, us, ur, gs, gr,
):
    nsec, nrow, ncol, nf, ns, nb, square = sizes
    rows, width = panel_ref.shape
    pw = anc_ref.shape[1]
    per = width // pw
    slots = rows // SW
    wb = SW // B
    tri = wb * (wb + 1) // 2
    part = tri * B // nrow
    tm = 256
    sec, row, col = lax.axis_index("sec"), lax.axis_index("row"), lax.axis_index("col")
    turn = sec if square else 0
    a, b = row // nb, row % nb
    f = a + turn * (b - a)
    s = b + turn * (a - b)
    cf = nb - turn * (nb - 1)
    cs = 1 + turn * (nb - 1)

    def at(fi, si):
        return fi * cf + si * cs

    def copy(src, dst, send, recv, where):
        return pltpu.make_async_remote_copy(
            src_ref=src, dst_ref=dst, send_sem=send, recv_sem=recv, device_id=where, device_id_type=MESH
        )

    has_left = (col > 0).astype(jnp.int32)
    has_right = (col < ncol - 1).astype(jnp.int32)
    barrier = pltpu.get_barrier_semaphore()
    for d in range(1, nrow):
        pl.semaphore_signal(barrier, inc=1, device_id={"row": (row + d) % nrow}, device_id_type=MESH)
    pl.semaphore_signal(barrier, inc=1, device_id={"sec": 1 - sec}, device_id_type=MESH)

    @pl.when(col > 0)
    def _():
        pl.semaphore_signal(barrier, inc=1, device_id={"col": col - 1}, device_id_type=MESH)

    @pl.when(col < ncol - 1)
    def _():
        pl.semaphore_signal(barrier, inc=1, device_id={"col": col + 1}, device_id_type=MESH)

    pl.semaphore_wait(barrier, nrow + has_left + has_right)

    mine = sec * ncol + col

    def piece_copy(src, p, way):
        where = ({"col": col - 1}, {"col": col + 1}, {"sec": 1 - sec})[way]
        return copy(src, anc.at[p], zs.at[p, way], zr.at[p], where)

    def opp_copy(src, d, e, k):
        return copy(
            src, opp.at[d - 1, e - 1, k], os_.at[d - 1, e - 1, k], or_.at[d - 1, e - 1, k],
            {"row": at((f + d) % nf, s)},
        )

    def pass_on(src, p):
        for d in range(1, nf):
            for e in range(1, ns):
                @pl.when(p // per == at((f + d) % nf, (s + e) % ns))
                def _():
                    opp_copy(src, d, e, p % per).start()

    def panel_copy(d, j):
        return copy(
            panel_ref.at[pl.ds(j * SW, SW)], pin.at[d - 1, j], ps.at[d - 1, j], pr.at[d - 1, j],
            {"row": at((f + d) % nf, s)},
        )

    def halves(src, p):
        high, low = split(src[...])
        ah[p] = high
        al[p] = low

    @pl.when(col > 0)
    def _():
        piece_copy(anc_ref, mine, 0).start()

    @pl.when(col < ncol - 1)
    def _():
        piece_copy(anc_ref, mine, 1).start()

    piece_copy(anc_ref, mine, 2).start()
    pass_on(anc_ref, mine)
    for j in range(slots):
        for d in range(1, nf):
            panel_copy(d, j).start()

    halves(anc_ref, mine)
    high, low = split(panel_ref[...])
    ph[0] = high
    plo[0] = low

    def from_left(t):
        p = mine - t
        piece_copy(anc_ref, p, 2).wait_recv()

        @pl.when(col < ncol - 1)
        def _():
            piece_copy(anc.at[p], p, 1).start()

        piece_copy(anc.at[p], p, 2).start()
        pass_on(anc.at[p], p)
        halves(anc.at[p], p)

    def from_right(t):
        p = mine + t
        piece_copy(anc_ref, p, 2).wait_recv()

        @pl.when(col > 0)
        def _():
            piece_copy(anc.at[p], p, 0).start()

        piece_copy(anc.at[p], p, 2).start()
        pass_on(anc.at[p], p)
        halves(anc.at[p], p)

    def from_partner(p):
        piece_copy(anc_ref, p, 2).wait_recv()
        pass_on(anc.at[p], p)
        halves(anc.at[p], p)

    other = (1 - sec) * ncol + col
    from_partner(other)

    def gather_step(t, carry):
        pl.when(col - t >= 0)(lambda: from_left(t))
        pl.when(col + t < ncol)(lambda: from_right(t))
        pl.when(col - t >= 0)(lambda: from_partner(other - t))
        pl.when(col + t < ncol)(lambda: from_partner(other + t))
        return carry

    lax.fori_loop(1, ncol, gather_step, 0)

    for j in range(slots):
        for d in range(1, nf):
            panel_copy(d, j).wait_recv()
            high, low = split(pin[d - 1, j])
            ph[d, pl.ds(j * SW, SW)] = high
            plo[d, pl.ds(j * SW, SW)] = low
    for d in range(1, nf):
        for e in range(1, ns):
            for k in range(per):
                opp_copy(anc_ref, d, e, k).wait_recv()
                high, low = split(opp[d - 1, e - 1, k])
                oh[d - 1, e - 1, k] = high
                ol[d - 1, e - 1, k] = low

    def q_copy(e, j):
        return copy(
            qsend.at[e - 1, j], qrecv.at[e - 1, j], qs.at[e - 1, j], qr.at[e - 1, j],
            {"row": at(f, (s + e) % ns)},
        )

    for j in range(slots):
        for e in range(1, ns):
            base = at(f, (s + e) % ns) * per

            def target(i, carry):
                r = pl.multiple_of(i * tm, tm)
                rr = pl.ds(pl.multiple_of(j * SW + r, tm), tm)
                for k in range(per):
                    acc = dot3(ph[0, rr], plo[0, rr], ah[base + k], al[base + k], NN)
                    for d in range(1, nf):
                        acc += dot3(ph[d, rr], plo[d, rr], oh[d - 1, e - 1, k], ol[d - 1, e - 1, k], NN)
                    qsend[e - 1, j, pl.ds(r, tm), pl.ds(k * pw, pw)] = acc
                return carry

            lax.fori_loop(0, SW // tm, target, 0)
            q_copy(e, j).start()

    def own(i, carry):
        rr = pl.ds(pl.multiple_of(i * tm, tm), tm)
        for k in range(per):
            p = at(f, s) * per + k
            prod_ref[rr, pl.ds(k * pw, pw)] = dot3(ph[0, rr], plo[0, rr], ah[p], al[p], NN)
        for d in range(1, nf):
            for k in range(per):
                p = at((f + nf - d) % nf, s) * per + k
                cols = pl.ds(k * pw, pw)
                prod_ref[rr] += dot3(ph[d, rr, cols], plo[d, rr, cols], ah[p], al[p], NT)
        return carry

    lax.fori_loop(0, rows // tm, own, 0)

    def u_copy(j, d):
        return copy(
            upack.at[j, pl.ds(pl.multiple_of(((row + d) % nrow) * part, 8), part)],
            urecv.at[j, d - 1], us.at[j, d - 1], ur.at[j, d - 1], {"row": (row + d) % nrow},
        )

    def g_copy(j, d):
        return copy(
            usum.at[j], ugat.at[j, d - 1], gs.at[j, d - 1], gr.at[j, d - 1], {"row": (row + d) % nrow}
        )

    for j in range(slots):
        jr = pl.ds(j * SW, SW)
        for e in range(1, ns):
            q_copy(e, j).wait_recv()
            prod_ref[jr] += qrecv[e - 1, j]
        spot = 0
        for i in range(wb):
            qh, ql = split(prod_ref[pl.ds(j * SW + i * B, B)])
            rest = pl.ds(j * SW + i * B, SW - i * B)
            line = dot3(qh, ql, ph[0, rest], plo[0, rest], NT)
            for k in range(i, wb):
                upack[j, pl.ds(spot * B, B)] = line[:, (k - i) * B:(k - i + 1) * B]
                spot += 1
        for d in range(1, nrow):
            u_copy(j, d).start()

    for j in range(slots):
        for d in range(1, nrow):
            u_copy(j, d).wait_recv()
        total = upack[j, pl.ds(pl.multiple_of(row * part, 8), part)]
        for d in range(1, nrow):
            total += urecv[j, d - 1]
        usum[j] = total
        for d in range(1, nrow):
            g_copy(j, d).start()

    for j in range(slots):
        for d in range(1, nrow):
            u_copy(j, d).wait_send()
        upack[j, pl.ds(pl.multiple_of(row * part, 8), part)] = usum[j]
        for d in range(1, nrow):
            g_copy(j, d).wait_recv()
            upack[j, pl.ds(pl.multiple_of(((row + nrow - d) % nrow) * part, 8), part)] = ugat[j, d - 1]
        spot = 0
        for i in range(wb):
            for k in range(i, wb):
                block = upack[j, pl.ds(spot * B, B)]
                upd_ref[pl.ds(j * SW + i * B, B), pl.ds(k * B, B)] = block
                if k > i:
                    upd_ref[pl.ds(j * SW + k * B, B), pl.ds(i * B, B)] = block.T
                spot += 1

    for j in range(slots):
        for d in range(1, nrow):
            g_copy(j, d).wait_send()
        for e in range(1, ns):
            q_copy(e, j).wait_send()
        for d in range(1, nf):
            panel_copy(d, j).wait_send()
    for d in range(1, nf):
        for e in range(1, ns):
            for k in range(per):
                opp_copy(anc_ref, d, e, k).wait_send()

    def drain(q, carry):
        p = sec * ncol + q
        pl.when(jnp.logical_and(q <= col, col < ncol - 1))(lambda: piece_copy(anc_ref, p, 1).wait_send())
        pl.when(jnp.logical_and(q >= col, col > 0))(lambda: piece_copy(anc_ref, p, 0).wait_send())
        piece_copy(anc_ref, p, 2).wait_send()
        return carry

    lax.fori_loop(0, ncol, drain, 0)


def exchange(sizes, anc_inverse, panel):
    nsec, nrow, ncol, nf, ns, nb, square = sizes
    rows, width = panel.shape
    pw = anc_inverse.shape[1]
    per = width // pw
    slots = rows // SW
    pieces = nsec * ncol
    wb = SW // B
    packed = wb * (wb + 1) // 2 * B
    part = packed // nrow
    vm = pltpu.VMEM
    dma = pltpu.SemaphoreType.DMA
    whole = pl.BlockSpec(memory_space=pltpu.VMEM)
    return pl.pallas_call(
        functools.partial(kernel, sizes),
        out_shape=(jax.ShapeDtypeStruct((rows, width), F32), jax.ShapeDtypeStruct((rows, SW), F32)),
        in_specs=[whole, whole],
        out_specs=(whole, whole),
        scratch_shapes=[
            vm((pieces, width, pw), F32),
            vm((pieces, width, pw), BF),
            vm((pieces, width, pw), BF),
            vm((nf, rows, width), BF),
            vm((nf, rows, width), BF),
            vm((nf - 1, slots, SW, width), F32),
            vm((nf - 1, ns - 1, per, width, pw), F32),
            vm((nf - 1, ns - 1, per, width, pw), BF),
            vm((nf - 1, ns - 1, per, width, pw), BF),
            vm((ns - 1, slots, SW, width), F32),
            vm((ns - 1, slots, SW, width), F32),
            vm((slots, packed, B), F32),
            vm((slots, nrow - 1, part, B), F32),
            vm((slots, part, B), F32),
            vm((slots, nrow - 1, part, B), F32),
            dma((pieces, 3)), dma((pieces,)),
            dma((nf - 1, slots)), dma((nf - 1, slots)),
            dma((nf - 1, ns - 1, per)), dma((nf - 1, ns - 1, per)),
            dma((ns - 1, slots)), dma((ns - 1, slots)),
            dma((slots, nrow - 1)), dma((slots, nrow - 1)),
            dma((slots, nrow - 1)), dma((slots, nrow - 1)),
        ],
        compiler_params=pltpu.CompilerParams(
            collective_id=0, has_side_effects=True, vmem_limit_bytes=60 * 1024 * 1024
        ),
    )(anc_inverse, panel)


def local(sizes, anc_inverse, panel, diag_inverse, widths, pattern):
    local_rows, rows_here = panel.shape
    slot_count = local_rows // SW
    slot_first = (lax.axis_index("sec") * lax.axis_size("col") + lax.axis_index("col")) * slot_count
    blocks = rows_here // B
    my_widths = lax.dynamic_slice_in_dim(widths, slot_first, slot_count)
    my_pattern = lax.dynamic_slice(
        pattern, (slot_first, lax.axis_index("row") * blocks), (slot_count, blocks)
    )
    block_mask = jnp.repeat(my_pattern.astype(F32), B, axis=1)
    position = jnp.arange(SW, dtype=jnp.int32)
    column_mask = (position[None, :] < my_widths[:, None] * B).astype(F32)
    mask = column_mask[:, :, None] * block_mask[:, None, :]
    masked = (panel.reshape(slot_count, SW, rows_here) * mask).reshape(local_rows, rows_here)
    product, update = exchange(sizes, anc_inverse, masked)
    product = product.reshape(slot_count, SW, rows_here) * mask
    pair_mask = column_mask[:, :, None] * column_mask[:, None, :]
    diag_block = (diag_inverse + update) * pair_mask.reshape(local_rows, SW)
    return (-product.reshape(local_rows, rows_here), diag_block)


def solution(mesh):
    shape = dict(mesh.shape)
    na, nb = factor(shape["row"])
    sizes = (shape["sec"], shape["row"], shape["col"], na, nb, nb, na == nb)
    in_specs = (
        P("row", ("sec", "col")),
        P(("sec", "col"), "row"),
        P(("sec", "col"), None),
        P(),
        P(),
    )
    out_specs = (P(("sec", "col"), "row"), P(("sec", "col"), None))
    return jax.shard_map(
        functools.partial(local, sizes), mesh=mesh, in_specs=in_specs, out_specs=out_specs, check_vma=False
    )
```

```python
import functools
import jax
import jax.numpy as jnp
from jax import lax
from jax.experimental import pallas as pl
from jax.experimental.pallas import tpu as pltpu
from jax.sharding import PartitionSpec as P

B = 128
SW = 512
F32 = jnp.float32
BF = jnp.bfloat16
MESH = pl.DeviceIdType.MESH
NN = (((1,), (0,)), ((), ()))
NT = (((1,), (1,)), ((), ()))


def split(value):
    high = value.astype(BF)
    return high, (value - high.astype(F32)).astype(BF)


def dot3(ah, al, bh, bl, dims):
    dot = functools.partial(lax.dot_general, dimension_numbers=dims, preferred_element_type=F32)
    return dot(ah, bh) + (dot(ah, bl) + dot(al, bh))


def factor(count):
    low = 1
    for value in range(1, count + 1):
        if count % value == 0 and value * value <= count:
            low = value
    return count // low, low


def kernel(
    sizes,
    anc_ref, panel_ref, diag_ref, widths_ref, pattern_ref, prod_ref, upd_ref,
    anc, ah, al, ph, plo, pin, opp, oh, ol, qsend, qrecv, upack, urecv, usum, ugat,
    zs, zr, ps, pr, os_, or_, qs, qr, us, ur, gs, gr, ds,
):
    nsec, nrow, ncol, nf, ns, nb, square = sizes
    rows, width = panel_ref.shape
    pw = anc_ref.shape[1]
    per = width // pw
    slots = rows // SW
    wb = SW // B
    tri = wb * (wb + 1) // 2
    part = tri * B // nrow
    tm = 256
    sec, row, col = lax.axis_index("sec"), lax.axis_index("row"), lax.axis_index("col")
    turn = sec if square else 0
    a, b = row // nb, row % nb
    f = a + turn * (b - a)
    s = b + turn * (a - b)
    cf = nb - turn * (nb - 1)
    cs = 1 + turn * (nb - 1)

    def at(fi, si):
        return fi * cf + si * cs

    def copy(src, dst, send, recv, where):
        return pltpu.make_async_remote_copy(
            src_ref=src, dst_ref=dst, send_sem=send, recv_sem=recv, device_id=where, device_id_type=MESH
        )

    first = (sec * ncol + col) * slots
    blocks = width // B
    fill = [widths_ref[first + j] for j in range(slots)]
    load_diag = pltpu.make_async_copy(diag_ref, upd_ref, ds)

    def inside(j, i):
        return jnp.where(fill[j] > i, 1.0, 0.0).astype(F32)

    def present(j, r, c):
        return pattern_ref[first + j, r * blocks + c].astype(F32)

    def keep(src, j, slot, r):
        for i in range(wb):
            here = pl.ds(j * SW + i * B, B)
            for c in range(blocks):
                cols = pl.ds(c * B, B)
                high, low = split(src(i, cols) * (inside(j, i) * present(j, r, c)))
                ph[slot, here, cols] = high
                plo[slot, here, cols] = low

    has_left = (col > 0).astype(jnp.int32)
    has_right = (col < ncol - 1).astype(jnp.int32)
    barrier = pltpu.get_barrier_semaphore()
    for d in range(1, nrow):
        pl.semaphore_signal(barrier, inc=1, device_id={"row": (row + d) % nrow}, device_id_type=MESH)
    pl.semaphore_signal(barrier, inc=1, device_id={"sec": 1 - sec}, device_id_type=MESH)

    @pl.when(col > 0)
    def _():
        pl.semaphore_signal(barrier, inc=1, device_id={"col": col - 1}, device_id_type=MESH)

    @pl.when(col < ncol - 1)
    def _():
        pl.semaphore_signal(barrier, inc=1, device_id={"col": col + 1}, device_id_type=MESH)

    pl.semaphore_wait(barrier, nrow + has_left + has_right)

    mine = sec * ncol + col

    def piece_copy(src, p, way):
        where = ({"col": col - 1}, {"col": col + 1}, {"sec": 1 - sec})[way]
        return copy(src, anc.at[p], zs.at[p, way], zr.at[p], where)

    def opp_copy(src, d, e, k):
        return copy(
            src, opp.at[d - 1, e - 1, k], os_.at[d - 1, e - 1, k], or_.at[d - 1, e - 1, k],
            {"row": at((f + d) % nf, s)},
        )

    def pass_on(src, p):
        for d in range(1, nf):
            for e in range(1, ns):
                @pl.when(p // per == at((f + d) % nf, (s + e) % ns))
                def _():
                    opp_copy(src, d, e, p % per).start()

    def panel_copy(d, j):
        return copy(
            panel_ref.at[pl.ds(j * SW, SW)], pin.at[d - 1, j], ps.at[d - 1, j], pr.at[d - 1, j],
            {"row": at((f + d) % nf, s)},
        )

    def halves(src, p):
        high, low = split(src[...])
        ah[p] = high
        al[p] = low

    def late(p):
        return p // per == row

    def send_mine():
        pl.when(col > 0)(lambda: piece_copy(anc_ref, mine, 0).start())
        pl.when(col < ncol - 1)(lambda: piece_copy(anc_ref, mine, 1).start())
        piece_copy(anc_ref, mine, 2).start()

    @pl.when(jnp.logical_not(late(mine)))
    def _():
        send_mine()
        pass_on(anc_ref, mine)

    for j in range(slots):
        for d in range(1, nf):
            panel_copy(d, j).start()

    load_diag.start()
    halves(anc_ref, mine)
    for j in range(slots):
        keep(lambda i, cols: panel_ref[pl.ds(j * SW + i * B, B), cols], j, 0, row)

    def from_left(t):
        p = mine - t
        piece_copy(anc_ref, p, 2).wait_recv()

        @pl.when(col < ncol - 1)
        def _():
            piece_copy(anc.at[p], p, 1).start()

        piece_copy(anc.at[p], p, 2).start()
        pass_on(anc.at[p], p)
        halves(anc.at[p], p)

    def from_right(t):
        p = mine + t
        piece_copy(anc_ref, p, 2).wait_recv()

        @pl.when(col > 0)
        def _():
            piece_copy(anc.at[p], p, 0).start()

        piece_copy(anc.at[p], p, 2).start()
        pass_on(anc.at[p], p)
        halves(anc.at[p], p)

    def from_partner(p):
        piece_copy(anc_ref, p, 2).wait_recv()
        pass_on(anc.at[p], p)
        halves(anc.at[p], p)

    other = (1 - sec) * ncol + col

    def gather(phase):
        def ready(p):
            return late(p) if phase else jnp.logical_not(late(p))

        pl.when(ready(other))(lambda: from_partner(other))

        def step(t, carry):
            left = col - t >= 0
            right = col + t < ncol
            pl.when(jnp.logical_and(left, ready(mine - t)))(lambda: from_left(t))
            pl.when(jnp.logical_and(right, ready(mine + t)))(lambda: from_right(t))
            pl.when(jnp.logical_and(left, ready(other - t)))(lambda: from_partner(other - t))
            pl.when(jnp.logical_and(right, ready(other + t)))(lambda: from_partner(other + t))
            return carry

        lax.fori_loop(1, ncol, step, 0)

    gather(0)
    pl.when(late(mine))(send_mine)

    for j in range(slots):
        for d in range(1, nf):
            panel_copy(d, j).wait_recv()
            keep(lambda i, cols: pin[d - 1, j, pl.ds(i * B, B), cols], j, d, at((f + nf - d) % nf, s))
    for d in range(1, nf):
        for e in range(1, ns):
            for k in range(per):
                opp_copy(anc_ref, d, e, k).wait_recv()
                high, low = split(opp[d - 1, e - 1, k])
                oh[d - 1, e - 1, k] = high
                ol[d - 1, e - 1, k] = low

    def q_copy(e, j):
        return copy(
            qsend.at[e - 1, j], qrecv.at[e - 1, j], qs.at[e - 1, j], qr.at[e - 1, j],
            {"row": at(f, (s + e) % ns)},
        )

    for j in range(slots):
        for e in range(1, ns):
            base = at(f, (s + e) % ns) * per

            def target(i, carry):
                r = pl.multiple_of(i * tm, tm)
                rr = pl.ds(pl.multiple_of(j * SW + r, tm), tm)
                for k in range(per):
                    acc = dot3(ph[0, rr], plo[0, rr], ah[base + k], al[base + k], NN)
                    for d in range(1, nf):
                        acc += dot3(ph[d, rr], plo[d, rr], oh[d - 1, e - 1, k], ol[d - 1, e - 1, k], NN)
                    qsend[e - 1, j, pl.ds(r, tm), pl.ds(k * pw, pw)] = acc
                return carry

            lax.fori_loop(0, SW // tm, target, 0)
            q_copy(e, j).start()

    def near(i, carry):
        rr = pl.ds(pl.multiple_of(i * tm, tm), tm)
        acc = jnp.zeros((tm, width), F32)
        for d in range(1, nf):
            for k in range(per):
                p = at((f + nf - d) % nf, s) * per + k
                cols = pl.ds(k * pw, pw)
                acc += dot3(ph[d, rr, cols], plo[d, rr, cols], ah[p], al[p], NT)
        prod_ref[rr] = acc
        return carry

    lax.fori_loop(0, rows // tm, near, 0)
    gather(1)

    def own(i, carry):
        rr = pl.ds(pl.multiple_of(i * tm, tm), tm)
        for k in range(per):
            p = row * per + k
            prod_ref[rr, pl.ds(k * pw, pw)] += dot3(ph[0, rr], plo[0, rr], ah[p], al[p], NN)
        return carry

    lax.fori_loop(0, rows // tm, own, 0)

    def u_copy(j, d):
        return copy(
            upack.at[j, pl.ds(pl.multiple_of(((row + d) % nrow) * part, 8), part)],
            urecv.at[j, d - 1], us.at[j, d - 1], ur.at[j, d - 1], {"row": (row + d) % nrow},
        )

    def g_copy(j, d):
        return copy(
            usum.at[j], ugat.at[j, d - 1], gs.at[j, d - 1], gr.at[j, d - 1], {"row": (row + d) % nrow}
        )

    for j in range(slots):
        jr = pl.ds(j * SW, SW)
        for e in range(1, ns):
            q_copy(e, j).wait_recv()
            prod_ref[jr] += qrecv[e - 1, j]
        spot = 0
        for i in range(wb):
            qh, ql = split(prod_ref[pl.ds(j * SW + i * B, B)])
            rest = pl.ds(j * SW + i * B, SW - i * B)
            line = dot3(qh, ql, ph[0, rest], plo[0, rest], NT)
            for k in range(i, wb):
                upack[j, pl.ds(spot * B, B)] = line[:, (k - i) * B:(k - i + 1) * B]
                spot += 1
        for d in range(1, nrow):
            u_copy(j, d).start()

    for j in range(slots):
        for i in range(wb):
            here = pl.ds(j * SW + i * B, B)
            for c in range(blocks):
                cols = pl.ds(c * B, B)
                prod_ref[here, cols] = prod_ref[here, cols] * -(inside(j, i) * present(j, row, c))

    for j in range(slots):
        for d in range(1, nrow):
            u_copy(j, d).wait_recv()
        total = upack[j, pl.ds(pl.multiple_of(row * part, 8), part)]
        for d in range(1, nrow):
            total += urecv[j, d - 1]
        usum[j] = total
        for d in range(1, nrow):
            g_copy(j, d).start()

    load_diag.wait()
    for j in range(slots):
        for d in range(1, nrow):
            u_copy(j, d).wait_send()
        upack[j, pl.ds(pl.multiple_of(row * part, 8), part)] = usum[j]
        for d in range(1, nrow):
            g_copy(j, d).wait_recv()
            upack[j, pl.ds(pl.multiple_of(((row + nrow - d) % nrow) * part, 8), part)] = ugat[j, d - 1]
        spot = 0
        for i in range(wb):
            for k in range(i, wb):
                block = upack[j, pl.ds(spot * B, B)]
                held = inside(j, k)
                upper = (pl.ds(j * SW + i * B, B), pl.ds(k * B, B))
                upd_ref[upper] = (upd_ref[upper] + block) * held
                if k > i:
                    lower = (pl.ds(j * SW + k * B, B), pl.ds(i * B, B))
                    upd_ref[lower] = (upd_ref[lower] + block.T) * held
                spot += 1

    for j in range(slots):
        for d in range(1, nrow):
            g_copy(j, d).wait_send()
        for e in range(1, ns):
            q_copy(e, j).wait_send()
        for d in range(1, nf):
            panel_copy(d, j).wait_send()
    for d in range(1, nf):
        for e in range(1, ns):
            for k in range(per):
                opp_copy(anc_ref, d, e, k).wait_send()

    def drain(q, carry):
        p = sec * ncol + q
        pl.when(jnp.logical_and(q <= col, col < ncol - 1))(lambda: piece_copy(anc_ref, p, 1).wait_send())
        pl.when(jnp.logical_and(q >= col, col > 0))(lambda: piece_copy(anc_ref, p, 0).wait_send())
        piece_copy(anc_ref, p, 2).wait_send()
        return carry

    lax.fori_loop(0, ncol, drain, 0)


def local(sizes, anc_inverse, panel, diag_inverse, widths, pattern):
    nsec, nrow, ncol, nf, ns, nb, square = sizes
    rows, width = panel.shape
    pw = anc_inverse.shape[1]
    per = width // pw
    slots = rows // SW
    pieces = nsec * ncol
    wb = SW // B
    packed = wb * (wb + 1) // 2 * B
    part = packed // nrow
    vm = pltpu.VMEM
    dma = pltpu.SemaphoreType.DMA
    whole = pl.BlockSpec(memory_space=pltpu.VMEM)
    scalar = pl.BlockSpec(memory_space=pltpu.SMEM)
    return pl.pallas_call(
        functools.partial(kernel, sizes),
        out_shape=(jax.ShapeDtypeStruct((rows, width), F32), jax.ShapeDtypeStruct((rows, SW), F32)),
        in_specs=[whole, whole, pl.BlockSpec(memory_space=pl.ANY), scalar, scalar],
        out_specs=(whole, whole),
        scratch_shapes=[
            vm((pieces, width, pw), F32),
            vm((pieces, width, pw), BF),
            vm((pieces, width, pw), BF),
            vm((nf, rows, width), BF),
            vm((nf, rows, width), BF),
            vm((nf - 1, slots, SW, width), F32),
            vm((nf - 1, ns - 1, per, width, pw), F32),
            vm((nf - 1, ns - 1, per, width, pw), BF),
            vm((nf - 1, ns - 1, per, width, pw), BF),
            vm((ns - 1, slots, SW, width), F32),
            vm((ns - 1, slots, SW, width), F32),
            vm((slots, packed, B), F32),
            vm((slots, nrow - 1, part, B), F32),
            vm((slots, part, B), F32),
            vm((slots, nrow - 1, part, B), F32),
            dma((pieces, 3)), dma((pieces,)),
            dma((nf - 1, slots)), dma((nf - 1, slots)),
            dma((nf - 1, ns - 1, per)), dma((nf - 1, ns - 1, per)),
            dma((ns - 1, slots)), dma((ns - 1, slots)),
            dma((slots, nrow - 1)), dma((slots, nrow - 1)),
            dma((slots, nrow - 1)), dma((slots, nrow - 1)),
            dma,
        ],
        compiler_params=pltpu.CompilerParams(
            collective_id=0, has_side_effects=True, vmem_limit_bytes=60 * 1024 * 1024
        ),
    )(anc_inverse, panel, diag_inverse, widths, pattern)


def solution(mesh):
    shape = dict(mesh.shape)
    na, nb = factor(shape["row"])
    sizes = (shape["sec"], shape["row"], shape["col"], na, nb, nb, na == nb)
    in_specs = (
        P("row", ("sec", "col")),
        P(("sec", "col"), "row"),
        P(("sec", "col"), None),
        P(),
        P(),
    )
    out_specs = (P(("sec", "col"), "row"), P(("sec", "col"), None))
    return jax.shard_map(
        functools.partial(local, sizes), mesh=mesh, in_specs=in_specs, out_specs=out_specs, check_vma=False
    )
```

```python
import functools
import jax
import jax.numpy as jnp
from jax import lax
from jax.experimental import pallas as pl
from jax.experimental.pallas import tpu as pltpu
from jax.sharding import PartitionSpec as P

B = 128
SW = 512
CHUNKS = 4
F32 = jnp.float32
BF = jnp.bfloat16
MESH = pl.DeviceIdType.MESH
NN = (((1,), (0,)), ((), ()))
NT = (((1,), (1,)), ((), ()))


def split(value):
    high = value.astype(BF)
    return high, (value - high.astype(F32)).astype(BF)


def dot3(ah, al, bh, bl, dims):
    dot = functools.partial(lax.dot_general, dimension_numbers=dims, preferred_element_type=F32)
    return dot(ah, bh) + (dot(ah, bl) + dot(al, bh))


def factor(count):
    low = 1
    for value in range(1, count + 1):
        if count % value == 0 and value * value <= count:
            low = value
    return count // low, low


class Group:
    def __init__(self, copies):
        self.copies = copies

    def start(self):
        for one in self.copies:
            one.start()

    def wait_recv(self):
        for one in self.copies:
            one.wait_recv()

    def wait_send(self):
        for one in self.copies:
            one.wait_send()


def kernel(
    sizes,
    anc_ref, panel_ref, diag_ref, widths_ref, pattern_ref, prod_ref, upd_ref,
    anc, ah, al, ph, plo, pin, opp, oh, ol, qsend, qrecv, upack, urecv, usum, ugat,
    zs, zr, ps, pr, os_, or_, qs, qr, us, ur, gs, gr, ds,
):
    nsec, nrow, ncol, nf, ns, nb, square = sizes
    rows, width = panel_ref.shape
    pw = anc_ref.shape[1]
    per = width // pw
    slots = rows // SW
    wb = SW // B
    tri = wb * (wb + 1) // 2
    part = tri * B // nrow
    tm = 256
    sec, row, col = lax.axis_index("sec"), lax.axis_index("row"), lax.axis_index("col")
    turn = sec if square else 0
    a, b = row // nb, row % nb
    f = a + turn * (b - a)
    s = b + turn * (a - b)
    cf = nb - turn * (nb - 1)
    cs = 1 + turn * (nb - 1)

    def at(fi, si):
        return fi * cf + si * cs

    def copy(src, dst, send, recv, where):
        return pltpu.make_async_remote_copy(
            src_ref=src, dst_ref=dst, send_sem=send, recv_sem=recv, device_id=where, device_id_type=MESH
        )

    first = (sec * ncol + col) * slots
    blocks = width // B
    fill = [widths_ref[first + j] for j in range(slots)]
    load_diag = pltpu.make_async_copy(diag_ref, upd_ref, ds)

    def inside(j, i):
        return jnp.where(fill[j] > i, 1.0, 0.0).astype(F32)

    def present(j, r, c):
        return pattern_ref[first + j, r * blocks + c].astype(F32)

    def keep(src, j, slot, r):
        for i in range(wb):
            here = pl.ds(j * SW + i * B, B)
            for c in range(blocks):
                cols = pl.ds(c * B, B)
                high, low = split(src(i, cols) * (inside(j, i) * present(j, r, c)))
                ph[slot, here, cols] = high
                plo[slot, here, cols] = low

    has_left = (col > 0).astype(jnp.int32)
    has_right = (col < ncol - 1).astype(jnp.int32)
    barrier = pltpu.get_barrier_semaphore()
    for d in range(1, nrow):
        pl.semaphore_signal(barrier, inc=1, device_id={"row": (row + d) % nrow}, device_id_type=MESH)
    pl.semaphore_signal(barrier, inc=1, device_id={"sec": 1 - sec}, device_id_type=MESH)

    @pl.when(col > 0)
    def _():
        pl.semaphore_signal(barrier, inc=1, device_id={"col": col - 1}, device_id_type=MESH)

    @pl.when(col < ncol - 1)
    def _():
        pl.semaphore_signal(barrier, inc=1, device_id={"col": col + 1}, device_id_type=MESH)

    pl.semaphore_wait(barrier, nrow + has_left + has_right)

    mine = sec * ncol + col

    def piece_copy(src, p, way):
        where = ({"col": col - 1}, {"col": col + 1}, {"sec": 1 - sec})[way]
        size = src.shape[0] // CHUNKS
        return Group([
            copy(
                src.at[pl.ds(c * size, size)], anc.at[p, pl.ds(c * size, size)],
                zs.at[p, way, c], zr.at[p, c], where,
            )
            for c in range(CHUNKS)
        ])

    def opp_copy(src, d, e, k):
        return copy(
            src, opp.at[d - 1, e - 1, k], os_.at[d - 1, e - 1, k], or_.at[d - 1, e - 1, k],
            {"row": at((f + d) % nf, s)},
        )

    def pass_on(src, p):
        for d in range(1, nf):
            for e in range(1, ns):
                @pl.when(p // per == at((f + d) % nf, (s + e) % ns))
                def _():
                    opp_copy(src, d, e, p % per).start()

    def panel_copy(d, j):
        return copy(
            panel_ref.at[pl.ds(j * SW, SW)], pin.at[d - 1, j], ps.at[d - 1, j], pr.at[d - 1, j],
            {"row": at((f + d) % nf, s)},
        )

    def halves(src, p):
        high, low = split(src[...])
        ah[p] = high
        al[p] = low

    def late(p):
        return p // per == row

    def send_mine():
        pl.when(col > 0)(lambda: piece_copy(anc_ref, mine, 0).start())
        pl.when(col < ncol - 1)(lambda: piece_copy(anc_ref, mine, 1).start())
        piece_copy(anc_ref, mine, 2).start()

    @pl.when(jnp.logical_not(late(mine)))
    def _():
        send_mine()
        pass_on(anc_ref, mine)

    for j in range(slots):
        for d in range(1, nf):
            panel_copy(d, j).start()

    load_diag.start()
    halves(anc_ref, mine)
    for j in range(slots):
        keep(lambda i, cols: panel_ref[pl.ds(j * SW + i * B, B), cols], j, 0, row)

    def relay(p, way, c, onward):
        piece_copy(anc_ref, p, way).copies[c].wait_recv()
        pl.when(onward)(lambda: piece_copy(anc.at[p], p, way).copies[c].start())
        piece_copy(anc.at[p], p, 2).copies[c].start()

    def settle(p):
        pass_on(anc.at[p], p)
        halves(anc.at[p], p)

    def from_partner(p):
        piece_copy(anc_ref, p, 2).wait_recv()
        pass_on(anc.at[p], p)
        halves(anc.at[p], p)

    other = (1 - sec) * ncol + col

    def gather(phase):
        def ready(p):
            return late(p) if phase else jnp.logical_not(late(p))

        def step(t, carry):
            left = jnp.logical_and(col - t >= 0, ready(mine - t))
            right = jnp.logical_and(col + t < ncol, ready(mine + t))
            for c in range(CHUNKS):
                pl.when(left)(lambda: relay(mine - t, 1, c, col < ncol - 1))
                pl.when(right)(lambda: relay(mine + t, 0, c, col > 0))
            pl.when(left)(lambda: settle(mine - t))
            pl.when(right)(lambda: settle(mine + t))
            partners(t)
            return carry

        def partners(t):
            left = jnp.logical_and(col - t >= 0, ready(other - t))
            right = jnp.logical_and(col + t < ncol, ready(other + t))
            pl.when(left)(lambda: from_partner(other - t))
            pl.when(jnp.logical_and(right, t > 0))(lambda: from_partner(other + t))

        partners(0)
        lax.fori_loop(1, ncol, step, 0)

    gather(0)
    pl.when(late(mine))(send_mine)

    for j in range(slots):
        for d in range(1, nf):
            panel_copy(d, j).wait_recv()
            keep(lambda i, cols: pin[d - 1, j, pl.ds(i * B, B), cols], j, d, at((f + nf - d) % nf, s))
    for d in range(1, nf):
        for e in range(1, ns):
            for k in range(per):
                opp_copy(anc_ref, d, e, k).wait_recv()
                high, low = split(opp[d - 1, e - 1, k])
                oh[d - 1, e - 1, k] = high
                ol[d - 1, e - 1, k] = low

    def q_copy(e, j):
        return copy(
            qsend.at[e - 1, j], qrecv.at[e - 1, j], qs.at[e - 1, j], qr.at[e - 1, j],
            {"row": at(f, (s + e) % ns)},
        )

    for j in range(slots):
        for e in range(1, ns):
            base = at(f, (s + e) % ns) * per

            def target(i, carry):
                r = pl.multiple_of(i * tm, tm)
                rr = pl.ds(pl.multiple_of(j * SW + r, tm), tm)
                for k in range(per):
                    acc = dot3(ph[0, rr], plo[0, rr], ah[base + k], al[base + k], NN)
                    for d in range(1, nf):
                        acc += dot3(ph[d, rr], plo[d, rr], oh[d - 1, e - 1, k], ol[d - 1, e - 1, k], NN)
                    qsend[e - 1, j, pl.ds(r, tm), pl.ds(k * pw, pw)] = acc
                return carry

            lax.fori_loop(0, SW // tm, target, 0)
            q_copy(e, j).start()

    def near(i, carry):
        rr = pl.ds(pl.multiple_of(i * tm, tm), tm)
        acc = jnp.zeros((tm, width), F32)
        for d in range(1, nf):
            for k in range(per):
                p = at((f + nf - d) % nf, s) * per + k
                cols = pl.ds(k * pw, pw)
                acc += dot3(ph[d, rr, cols], plo[d, rr, cols], ah[p], al[p], NT)
        prod_ref[rr] = acc
        return carry

    lax.fori_loop(0, rows // tm, near, 0)
    gather(1)

    def own(i, carry):
        rr = pl.ds(pl.multiple_of(i * tm, tm), tm)
        for k in range(per):
            p = row * per + k
            prod_ref[rr, pl.ds(k * pw, pw)] += dot3(ph[0, rr], plo[0, rr], ah[p], al[p], NN)
        return carry

    lax.fori_loop(0, rows // tm, own, 0)

    def u_copy(j, d):
        return copy(
            upack.at[j, pl.ds(pl.multiple_of(((row + d) % nrow) * part, 8), part)],
            urecv.at[j, d - 1], us.at[j, d - 1], ur.at[j, d - 1], {"row": (row + d) % nrow},
        )

    def g_copy(j, d):
        return copy(
            usum.at[j], ugat.at[j, d - 1], gs.at[j, d - 1], gr.at[j, d - 1], {"row": (row + d) % nrow}
        )

    for j in range(slots):
        jr = pl.ds(j * SW, SW)
        for e in range(1, ns):
            q_copy(e, j).wait_recv()
            prod_ref[jr] += qrecv[e - 1, j]
        spot = 0
        for i in range(wb):
            qh, ql = split(prod_ref[pl.ds(j * SW + i * B, B)])
            rest = pl.ds(j * SW + i * B, SW - i * B)
            line = dot3(qh, ql, ph[0, rest], plo[0, rest], NT)
            for k in range(i, wb):
                upack[j, pl.ds(spot * B, B)] = line[:, (k - i) * B:(k - i + 1) * B]
                spot += 1
        for d in range(1, nrow):
            u_copy(j, d).start()

    for j in range(slots):
        for i in range(wb):
            here = pl.ds(j * SW + i * B, B)
            for c in range(blocks):
                cols = pl.ds(c * B, B)
                prod_ref[here, cols] = prod_ref[here, cols] * -(inside(j, i) * present(j, row, c))

    for j in range(slots):
        for d in range(1, nrow):
            u_copy(j, d).wait_recv()
        total = upack[j, pl.ds(pl.multiple_of(row * part, 8), part)]
        for d in range(1, nrow):
            total += urecv[j, d - 1]
        usum[j] = total
        for d in range(1, nrow):
            g_copy(j, d).start()

    load_diag.wait()
    for j in range(slots):
        for d in range(1, nrow):
            u_copy(j, d).wait_send()
        upack[j, pl.ds(pl.multiple_of(row * part, 8), part)] = usum[j]
        for d in range(1, nrow):
            g_copy(j, d).wait_recv()
            upack[j, pl.ds(pl.multiple_of(((row + nrow - d) % nrow) * part, 8), part)] = ugat[j, d - 1]
        spot = 0
        for i in range(wb):
            for k in range(i, wb):
                block = upack[j, pl.ds(spot * B, B)]
                held = inside(j, k)
                upper = (pl.ds(j * SW + i * B, B), pl.ds(k * B, B))
                upd_ref[upper] = (upd_ref[upper] + block) * held
                if k > i:
                    lower = (pl.ds(j * SW + k * B, B), pl.ds(i * B, B))
                    upd_ref[lower] = (upd_ref[lower] + block.T) * held
                spot += 1

    for j in range(slots):
        for d in range(1, nrow):
            g_copy(j, d).wait_send()
        for e in range(1, ns):
            q_copy(e, j).wait_send()
        for d in range(1, nf):
            panel_copy(d, j).wait_send()
    for d in range(1, nf):
        for e in range(1, ns):
            for k in range(per):
                opp_copy(anc_ref, d, e, k).wait_send()

    def drain(q, carry):
        p = sec * ncol + q
        pl.when(jnp.logical_and(q <= col, col < ncol - 1))(lambda: piece_copy(anc_ref, p, 1).wait_send())
        pl.when(jnp.logical_and(q >= col, col > 0))(lambda: piece_copy(anc_ref, p, 0).wait_send())
        piece_copy(anc_ref, p, 2).wait_send()
        return carry

    lax.fori_loop(0, ncol, drain, 0)


def local(sizes, anc_inverse, panel, diag_inverse, widths, pattern):
    nsec, nrow, ncol, nf, ns, nb, square = sizes
    rows, width = panel.shape
    pw = anc_inverse.shape[1]
    per = width // pw
    slots = rows // SW
    pieces = nsec * ncol
    wb = SW // B
    packed = wb * (wb + 1) // 2 * B
    part = packed // nrow
    vm = pltpu.VMEM
    dma = pltpu.SemaphoreType.DMA
    whole = pl.BlockSpec(memory_space=pltpu.VMEM)
    scalar = pl.BlockSpec(memory_space=pltpu.SMEM)
    return pl.pallas_call(
        functools.partial(kernel, sizes),
        out_shape=(jax.ShapeDtypeStruct((rows, width), F32), jax.ShapeDtypeStruct((rows, SW), F32)),
        in_specs=[whole, whole, pl.BlockSpec(memory_space=pl.ANY), scalar, scalar],
        out_specs=(whole, whole),
        scratch_shapes=[
            vm((pieces, width, pw), F32),
            vm((pieces, width, pw), BF),
            vm((pieces, width, pw), BF),
            vm((nf, rows, width), BF),
            vm((nf, rows, width), BF),
            vm((nf - 1, slots, SW, width), F32),
            vm((nf - 1, ns - 1, per, width, pw), F32),
            vm((nf - 1, ns - 1, per, width, pw), BF),
            vm((nf - 1, ns - 1, per, width, pw), BF),
            vm((ns - 1, slots, SW, width), F32),
            vm((ns - 1, slots, SW, width), F32),
            vm((slots, packed, B), F32),
            vm((slots, nrow - 1, part, B), F32),
            vm((slots, part, B), F32),
            vm((slots, nrow - 1, part, B), F32),
            dma((pieces, 3, CHUNKS)), dma((pieces, CHUNKS)),
            dma((nf - 1, slots)), dma((nf - 1, slots)),
            dma((nf - 1, ns - 1, per)), dma((nf - 1, ns - 1, per)),
            dma((ns - 1, slots)), dma((ns - 1, slots)),
            dma((slots, nrow - 1)), dma((slots, nrow - 1)),
            dma((slots, nrow - 1)), dma((slots, nrow - 1)),
            dma,
        ],
        compiler_params=pltpu.CompilerParams(
            collective_id=0, has_side_effects=True, vmem_limit_bytes=60 * 1024 * 1024
        ),
    )(anc_inverse, panel, diag_inverse, widths, pattern)


def solution(mesh):
    shape = dict(mesh.shape)
    na, nb = factor(shape["row"])
    sizes = (shape["sec"], shape["row"], shape["col"], na, nb, nb, na == nb)
    in_specs = (
        P("row", ("sec", "col")),
        P(("sec", "col"), "row"),
        P(("sec", "col"), None),
        P(),
        P(),
    )
    out_specs = (P(("sec", "col"), "row"), P(("sec", "col"), None))
    return jax.shard_map(
        functools.partial(local, sizes), mesh=mesh, in_specs=in_specs, out_specs=out_specs, check_vma=False
    )
```

```python
import functools
import jax
import jax.numpy as jnp
from jax import lax
from jax.experimental import pallas as pl
from jax.experimental.pallas import tpu as pltpu
from jax.sharding import PartitionSpec as P

B = 128
SW = 512
CHUNKS = 8
F32 = jnp.float32
BF = jnp.bfloat16
MESH = pl.DeviceIdType.MESH
NN = (((1,), (0,)), ((), ()))
NT = (((1,), (1,)), ((), ()))


def split(value):
    high = value.astype(BF)
    return high, (value - high.astype(F32)).astype(BF)


def dot3(ah, al, bh, bl, dims):
    dot = functools.partial(lax.dot_general, dimension_numbers=dims, preferred_element_type=F32)
    return dot(ah, bh) + (dot(ah, bl) + dot(al, bh))


def factor(count):
    low = 1
    for value in range(1, count + 1):
        if count % value == 0 and value * value <= count:
            low = value
    return count // low, low


class Group:
    def __init__(self, copies):
        self.copies = copies

    def start(self):
        for one in self.copies:
            one.start()

    def wait_recv(self):
        for one in self.copies:
            one.wait_recv()

    def wait_send(self):
        for one in self.copies:
            one.wait_send()


def kernel(
    sizes,
    anc_ref, panel_ref, diag_ref, widths_ref, pattern_ref, prod_ref, upd_ref,
    anc, ah, al, ph, plo, pin, opp, oh, ol, qsend, qrecv, upack, urecv, usum, ugat,
    zs, zr, ps, pr, os_, or_, qs, qr, us, ur, gs, gr, ds,
):
    nsec, nrow, ncol, nf, ns, nb, square = sizes
    rows, width = panel_ref.shape
    pw = anc_ref.shape[1]
    per = width // pw
    slots = rows // SW
    wb = SW // B
    tri = wb * (wb + 1) // 2
    part = tri * B // nrow
    tm = 256
    sec, row, col = lax.axis_index("sec"), lax.axis_index("row"), lax.axis_index("col")
    turn = sec if square else 0
    a, b = row // nb, row % nb
    f = a + turn * (b - a)
    s = b + turn * (a - b)
    cf = nb - turn * (nb - 1)
    cs = 1 + turn * (nb - 1)

    def at(fi, si):
        return fi * cf + si * cs

    def copy(src, dst, send, recv, where):
        return pltpu.make_async_remote_copy(
            src_ref=src, dst_ref=dst, send_sem=send, recv_sem=recv, device_id=where, device_id_type=MESH
        )

    first = (sec * ncol + col) * slots
    blocks = width // B
    fill = [widths_ref[first + j] for j in range(slots)]
    load_diag = pltpu.make_async_copy(diag_ref, upd_ref, ds)

    def inside(j, i):
        return jnp.where(fill[j] > i, 1.0, 0.0).astype(F32)

    def present(j, r, c):
        return pattern_ref[first + j, r * blocks + c].astype(F32)

    def keep(src, j, slot, r):
        for i in range(wb):
            here = pl.ds(j * SW + i * B, B)
            for c in range(blocks):
                cols = pl.ds(c * B, B)
                high, low = split(src(i, cols) * (inside(j, i) * present(j, r, c)))
                ph[slot, here, cols] = high
                plo[slot, here, cols] = low

    has_left = (col > 0).astype(jnp.int32)
    has_right = (col < ncol - 1).astype(jnp.int32)
    barrier = pltpu.get_barrier_semaphore()
    for d in range(1, nrow):
        pl.semaphore_signal(barrier, inc=1, device_id={"row": (row + d) % nrow}, device_id_type=MESH)
    pl.semaphore_signal(barrier, inc=1, device_id={"sec": 1 - sec}, device_id_type=MESH)

    @pl.when(col > 0)
    def _():
        pl.semaphore_signal(barrier, inc=1, device_id={"col": col - 1}, device_id_type=MESH)

    @pl.when(col < ncol - 1)
    def _():
        pl.semaphore_signal(barrier, inc=1, device_id={"col": col + 1}, device_id_type=MESH)

    pl.semaphore_wait(barrier, nrow + has_left + has_right)

    mine = sec * ncol + col

    def piece_copy(src, p, way):
        where = ({"col": col - 1}, {"col": col + 1}, {"sec": 1 - sec})[way]
        size = src.shape[0] // CHUNKS
        return Group([
            copy(
                src.at[pl.ds(c * size, size)], anc.at[p, pl.ds(c * size, size)],
                zs.at[p, way, c], zr.at[p, c], where,
            )
            for c in range(CHUNKS)
        ])

    def opp_copy(src, d, e, k):
        return copy(
            src, opp.at[d - 1, e - 1, k], os_.at[d - 1, e - 1, k], or_.at[d - 1, e - 1, k],
            {"row": at((f + d) % nf, s)},
        )

    def pass_on(src, p):
        for d in range(1, nf):
            for e in range(1, ns):
                @pl.when(p // per == at((f + d) % nf, (s + e) % ns))
                def _():
                    opp_copy(src, d, e, p % per).start()

    def panel_copy(d, j):
        return copy(
            panel_ref.at[pl.ds(j * SW, SW)], pin.at[d - 1, j], ps.at[d - 1, j], pr.at[d - 1, j],
            {"row": at((f + d) % nf, s)},
        )

    def halves(src, p):
        high, low = split(src[...])
        ah[p] = high
        al[p] = low

    def late(p):
        return p // per == row

    def send_mine():
        pl.when(col > 0)(lambda: piece_copy(anc_ref, mine, 0).start())
        pl.when(col < ncol - 1)(lambda: piece_copy(anc_ref, mine, 1).start())
        piece_copy(anc_ref, mine, 2).start()

    @pl.when(jnp.logical_not(late(mine)))
    def _():
        send_mine()
        pass_on(anc_ref, mine)

    for j in range(slots):
        for d in range(1, nf):
            panel_copy(d, j).start()

    load_diag.start()
    halves(anc_ref, mine)
    for j in range(slots):
        keep(lambda i, cols: panel_ref[pl.ds(j * SW + i * B, B), cols], j, 0, row)

    def relay(p, way, c, onward):
        piece_copy(anc_ref, p, way).copies[c].wait_recv()
        pl.when(onward)(lambda: piece_copy(anc.at[p], p, way).copies[c].start())
        piece_copy(anc.at[p], p, 2).copies[c].start()

    def settle(p):
        pass_on(anc.at[p], p)
        halves(anc.at[p], p)

    def from_partner(p):
        piece_copy(anc_ref, p, 2).wait_recv()
        pass_on(anc.at[p], p)
        halves(anc.at[p], p)

    other = (1 - sec) * ncol + col

    def gather(phase):
        def ready(p):
            return late(p) if phase else jnp.logical_not(late(p))

        def step(t, carry):
            left = jnp.logical_and(col - t >= 0, ready(mine - t))
            right = jnp.logical_and(col + t < ncol, ready(mine + t))
            for c in range(CHUNKS):
                pl.when(left)(lambda: relay(mine - t, 1, c, col < ncol - 1))
                pl.when(right)(lambda: relay(mine + t, 0, c, col > 0))
            pl.when(left)(lambda: settle(mine - t))
            pl.when(right)(lambda: settle(mine + t))
            partners(t)
            return carry

        def partners(t):
            left = jnp.logical_and(col - t >= 0, ready(other - t))
            right = jnp.logical_and(col + t < ncol, ready(other + t))
            pl.when(left)(lambda: from_partner(other - t))
            pl.when(jnp.logical_and(right, t > 0))(lambda: from_partner(other + t))

        partners(0)
        lax.fori_loop(1, ncol, step, 0)

    gather(0)
    pl.when(late(mine))(send_mine)

    for j in range(slots):
        for d in range(1, nf):
            panel_copy(d, j).wait_recv()
            keep(lambda i, cols: pin[d - 1, j, pl.ds(i * B, B), cols], j, d, at((f + nf - d) % nf, s))
    for d in range(1, nf):
        for e in range(1, ns):
            for k in range(per):
                opp_copy(anc_ref, d, e, k).wait_recv()
                high, low = split(opp[d - 1, e - 1, k])
                oh[d - 1, e - 1, k] = high
                ol[d - 1, e - 1, k] = low

    def q_copy(e, j):
        return copy(
            qsend.at[e - 1, j], qrecv.at[e - 1, j], qs.at[e - 1, j], qr.at[e - 1, j],
            {"row": at(f, (s + e) % ns)},
        )

    for j in range(slots):
        for e in range(1, ns):
            base = at(f, (s + e) % ns) * per

            def target(i, carry):
                r = pl.multiple_of(i * tm, tm)
                rr = pl.ds(pl.multiple_of(j * SW + r, tm), tm)
                for k in range(per):
                    acc = dot3(ph[0, rr], plo[0, rr], ah[base + k], al[base + k], NN)
                    for d in range(1, nf):
                        acc += dot3(ph[d, rr], plo[d, rr], oh[d - 1, e - 1, k], ol[d - 1, e - 1, k], NN)
                    qsend[e - 1, j, pl.ds(r, tm), pl.ds(k * pw, pw)] = acc
                return carry

            lax.fori_loop(0, SW // tm, target, 0)
            q_copy(e, j).start()

    def near(i, carry):
        rr = pl.ds(pl.multiple_of(i * tm, tm), tm)
        acc = jnp.zeros((tm, width), F32)
        for d in range(1, nf):
            for k in range(per):
                p = at((f + nf - d) % nf, s) * per + k
                cols = pl.ds(k * pw, pw)
                acc += dot3(ph[d, rr, cols], plo[d, rr, cols], ah[p], al[p], NT)
        prod_ref[rr] = acc
        return carry

    lax.fori_loop(0, rows // tm, near, 0)
    gather(1)

    def own(i, carry):
        rr = pl.ds(pl.multiple_of(i * tm, tm), tm)
        for k in range(per):
            p = row * per + k
            prod_ref[rr, pl.ds(k * pw, pw)] += dot3(ph[0, rr], plo[0, rr], ah[p], al[p], NN)
        return carry

    lax.fori_loop(0, rows // tm, own, 0)

    def u_copy(j, d):
        return copy(
            upack.at[j, pl.ds(pl.multiple_of(((row + d) % nrow) * part, 8), part)],
            urecv.at[j, d - 1], us.at[j, d - 1], ur.at[j, d - 1], {"row": (row + d) % nrow},
        )

    def g_copy(j, d):
        return copy(
            usum.at[j], ugat.at[j, d - 1], gs.at[j, d - 1], gr.at[j, d - 1], {"row": (row + d) % nrow}
        )

    for j in range(slots):
        jr = pl.ds(j * SW, SW)
        for e in range(1, ns):
            q_copy(e, j).wait_recv()
            prod_ref[jr] += qrecv[e - 1, j]
        spot = 0
        for i in range(wb):
            qh, ql = split(prod_ref[pl.ds(j * SW + i * B, B)])
            rest = pl.ds(j * SW + i * B, SW - i * B)
            line = dot3(qh, ql, ph[0, rest], plo[0, rest], NT)
            for k in range(i, wb):
                upack[j, pl.ds(spot * B, B)] = line[:, (k - i) * B:(k - i + 1) * B]
                spot += 1
        for d in range(1, nrow):
            u_copy(j, d).start()

    for j in range(slots):
        for i in range(wb):
            here = pl.ds(j * SW + i * B, B)
            for c in range(blocks):
                cols = pl.ds(c * B, B)
                prod_ref[here, cols] = prod_ref[here, cols] * -(inside(j, i) * present(j, row, c))

    for j in range(slots):
        for d in range(1, nrow):
            u_copy(j, d).wait_recv()
        total = upack[j, pl.ds(pl.multiple_of(row * part, 8), part)]
        for d in range(1, nrow):
            total += urecv[j, d - 1]
        usum[j] = total
        for d in range(1, nrow):
            g_copy(j, d).start()

    load_diag.wait()
    for j in range(slots):
        for d in range(1, nrow):
            u_copy(j, d).wait_send()
        upack[j, pl.ds(pl.multiple_of(row * part, 8), part)] = usum[j]
        for d in range(1, nrow):
            g_copy(j, d).wait_recv()
            upack[j, pl.ds(pl.multiple_of(((row + nrow - d) % nrow) * part, 8), part)] = ugat[j, d - 1]
        spot = 0
        for i in range(wb):
            for k in range(i, wb):
                block = upack[j, pl.ds(spot * B, B)]
                held = inside(j, k)
                upper = (pl.ds(j * SW + i * B, B), pl.ds(k * B, B))
                upd_ref[upper] = (upd_ref[upper] + block) * held
                if k > i:
                    lower = (pl.ds(j * SW + k * B, B), pl.ds(i * B, B))
                    upd_ref[lower] = (upd_ref[lower] + block.T) * held
                spot += 1

    for j in range(slots):
        for d in range(1, nrow):
            g_copy(j, d).wait_send()
        for e in range(1, ns):
            q_copy(e, j).wait_send()
        for d in range(1, nf):
            panel_copy(d, j).wait_send()
    for d in range(1, nf):
        for e in range(1, ns):
            for k in range(per):
                opp_copy(anc_ref, d, e, k).wait_send()

    def drain(q, carry):
        p = sec * ncol + q
        pl.when(jnp.logical_and(q <= col, col < ncol - 1))(lambda: piece_copy(anc_ref, p, 1).wait_send())
        pl.when(jnp.logical_and(q >= col, col > 0))(lambda: piece_copy(anc_ref, p, 0).wait_send())
        piece_copy(anc_ref, p, 2).wait_send()
        return carry

    lax.fori_loop(0, ncol, drain, 0)


def local(sizes, anc_inverse, panel, diag_inverse, widths, pattern):
    nsec, nrow, ncol, nf, ns, nb, square = sizes
    rows, width = panel.shape
    pw = anc_inverse.shape[1]
    per = width // pw
    slots = rows // SW
    pieces = nsec * ncol
    wb = SW // B
    packed = wb * (wb + 1) // 2 * B
    part = packed // nrow
    vm = pltpu.VMEM
    dma = pltpu.SemaphoreType.DMA
    whole = pl.BlockSpec(memory_space=pltpu.VMEM)
    scalar = pl.BlockSpec(memory_space=pltpu.SMEM)
    return pl.pallas_call(
        functools.partial(kernel, sizes),
        out_shape=(jax.ShapeDtypeStruct((rows, width), F32), jax.ShapeDtypeStruct((rows, SW), F32)),
        in_specs=[whole, whole, pl.BlockSpec(memory_space=pl.ANY), scalar, scalar],
        out_specs=(whole, whole),
        scratch_shapes=[
            vm((pieces, width, pw), F32),
            vm((pieces, width, pw), BF),
            vm((pieces, width, pw), BF),
            vm((nf, rows, width), BF),
            vm((nf, rows, width), BF),
            vm((nf - 1, slots, SW, width), F32),
            vm((nf - 1, ns - 1, per, width, pw), F32),
            vm((nf - 1, ns - 1, per, width, pw), BF),
            vm((nf - 1, ns - 1, per, width, pw), BF),
            vm((ns - 1, slots, SW, width), F32),
            vm((ns - 1, slots, SW, width), F32),
            vm((slots, packed, B), F32),
            vm((slots, nrow - 1, part, B), F32),
            vm((slots, part, B), F32),
            vm((slots, nrow - 1, part, B), F32),
            dma((pieces, 3, CHUNKS)), dma((pieces, CHUNKS)),
            dma((nf - 1, slots)), dma((nf - 1, slots)),
            dma((nf - 1, ns - 1, per)), dma((nf - 1, ns - 1, per)),
            dma((ns - 1, slots)), dma((ns - 1, slots)),
            dma((slots, nrow - 1)), dma((slots, nrow - 1)),
            dma((slots, nrow - 1)), dma((slots, nrow - 1)),
            dma,
        ],
        compiler_params=pltpu.CompilerParams(
            collective_id=0, has_side_effects=True, vmem_limit_bytes=60 * 1024 * 1024
        ),
    )(anc_inverse, panel, diag_inverse, widths, pattern)


def solution(mesh):
    shape = dict(mesh.shape)
    na, nb = factor(shape["row"])
    sizes = (shape["sec"], shape["row"], shape["col"], na, nb, nb, na == nb)
    in_specs = (
        P("row", ("sec", "col")),
        P(("sec", "col"), "row"),
        P(("sec", "col"), None),
        P(),
        P(),
    )
    out_specs = (P(("sec", "col"), "row"), P(("sec", "col"), None))
    return jax.shard_map(
        functools.partial(local, sizes), mesh=mesh, in_specs=in_specs, out_specs=out_specs, check_vma=False
    )
```
